32 devices in a mesh: line: 8 (over z, x), row: 4 (over y, core).
Axes of the slice: x: 2, y: 2, z: 4, core: 2. Of those that a mesh axis runs over, the one named last changes fastest.
Arguments:
- scalar_field: float32 [2048, 64, 512], P('line', None, 'row'), may hold values from -24 to 24
- cross_coef: float32 [2048, 64, 512], P('line', None, 'row'), may hold values from 0.03 to 0.24
- coupling: float32 [2048, 64, 512], P('line', None, 'row'), may hold values from 2000 to 20000
Outputs:
- solution: float32 [2048, 64, 512], P('line', None, 'row')
The draws below stay inside these ranges and needn't reach their ends.
All inputs are finite; a program needn't handle non-finite values.
Results may differ from the reference program's by a relative error of at most 0.003.
Values sent between devices are 32-bit elements; how exact they have to be, the bound alone decides.
A program may use at most 192 MiB of HBM per device.

```python
import math
import jax
import jax.numpy as jnp
from jax import lax

PTS = 2048
DEPTH = 64
NROWS = 512


def level_of(key, shape, split, least, high):
    def one(dim, shards_of):
        heights = jax.random.uniform(jax.random.fold_in(jax.random.fold_in(key, 6), dim), (shards_of,), jnp.float32, least / len(split), high / len(split))
        return jnp.repeat(jnp.exp(heights), shape[dim] // shards_of).reshape((-1,) + (1,) * (len(shape) - dim - 1))

    factor_of = one(*split[0])
    for cut in split[1:]:
        factor_of = factor_of * one(*cut)
    return factor_of


def bell_draw(own_key, shape, width, most, pieces=(), kind=jnp.bfloat16):
    loudness = level_of(own_key, shape, pieces, -0.22, 0.18) if pieces else 1.0
    values = jax.random.normal(own_key, shape, jnp.float32) * width * loudness
    return jnp.minimum(jnp.maximum(values, -most), most).astype(kind)


def setup_inputs(seed: int = 0) -> dict:
    key_list = jax.random.split(jax.random.key(seed), 4)
    scalar_field = bell_draw(key_list[0], (PTS, DEPTH, NROWS), 4.0, 24.0, ((0, 8), (2, 4)), jnp.float32)
    cross_coef = jnp.clip(jnp.exp(math.log(0.24) - 2.0794415 * jax.random.uniform(key_list[1], (PTS, DEPTH, NROWS), jnp.float32) ** level_of(key_list[1], (PTS, DEPTH, NROWS), ((0, 8), (2, 4)), -0.2, 0.2)), 0.03, 0.24)
    coupling = jnp.clip(jnp.exp(math.log(20000.0) - 2.3025851 * jax.random.uniform(key_list[2], (PTS, DEPTH, NROWS), jnp.float32) ** level_of(key_list[2], (PTS, DEPTH, NROWS), ((0, 8), (2, 4)), -0.2, 0.2)), 2000.0, 20000.0)
    return {"scalar_field": scalar_field, "cross_coef": cross_coef, "coupling": coupling}


def sweep_solve(sub_band, main_band, super_band, source):
    def forward(state_pair, stacked):
        factor, partial_sol = state_pair
        below, middle, above, source_row = stacked
        pivot_value = middle - below * factor
        new_factor = above / pivot_value
        new_partial = (source_row - below * partial_sol) / pivot_value
        return (new_factor, new_partial), (new_factor, new_partial)

    initial = (jnp.zeros_like(main_band[0]), jnp.zeros_like(source[0]))
    ignored, (factors, partials) = lax.scan(forward, initial, (sub_band, main_band, super_band, source))

    def backward(following, stacked):
        factor, partial_sol = stacked
        solved_value = partial_sol - factor * following
        return solved_value, solved_value

    ignored_too, values = lax.scan(backward, jnp.zeros_like(source[0]), (factors, partials), reverse=True)
    return values


def reference(scalar_field, cross_coef, coupling):
    padded = jnp.pad(scalar_field, ((0, 0), (1, 1), (1, 1)))

    def one_plane(plane_index):
        window = lax.dynamic_slice_in_dim(padded, plane_index, 3, 1)
        middle = window[:, 1, 1:-1]
        beside_all = window[:, 0, 1:-1] + window[:, 2, 1:-1] + window[:, 1, 2:] + window[:, 1, :-2]
        cross_plane = lax.dynamic_index_in_dim(cross_coef, plane_index, 1, False)
        face_plane = lax.dynamic_index_in_dim(coupling, plane_index, 1, False)
        explicit_part = middle + cross_plane * (beside_all - 4.0 * middle)
        next_face = jnp.roll(face_plane, -1, axis=0)
        return sweep_solve(-face_plane, 1.0 + face_plane + next_face, -next_face, explicit_part)

    planes = lax.map(one_plane, jnp.arange(DEPTH, dtype=jnp.int32))
    return jnp.moveaxis(planes, 0, 1)
```

```python
import functools

import jax
import jax.numpy as jnp
from jax import lax
from jax.experimental import pallas as pl
from jax.experimental.pallas import tpu as pltpu
from jax.sharding import PartitionSpec as P

F32 = jnp.float32
ANY = pl.BlockSpec(memory_space=pl.ANY)
VMEM = pl.BlockSpec(memory_space=pltpu.VMEM)


def lane_index(shape):
    return lax.broadcasted_iota(jnp.int32, shape, 1)


def pack_kernel(chunks, field, low, high, held, sems):
    points, depth, rows = held.shape
    step = points // chunks
    group = min(rows, points)
    copies = []
    for n in range(chunks):
        span = pl.ds(n * step, step)
        copy = pltpu.make_async_copy(field.at[span], held.at[span], sems.at[n])
        copy.start()
        copies.append(copy)
    lanes = lane_index((depth, rows))
    for n in range(chunks):
        copies[n].wait()
        base = n * step
        block, offset = base // group, base % group

        def body(k, state):
            first, last = state
            place = offset + k
            turned = pltpu.roll(held[base + k], place, 1)
            before = jnp.where(place == 0, rows - 1, place - 1)
            return jnp.where(lanes == place, turned, first), jnp.where(lanes == before, turned, last)

        if offset == 0:
            state = (jnp.zeros((depth, rows), F32), jnp.zeros((depth, rows), F32))
        state = lax.fori_loop(0, step, body, state, unroll=4)
        if offset + step == group:
            low[block], high[block] = state


def pack_edges(field):
    points, depth, rows = field.shape
    chunks = 8
    blocks = max(1, points // rows)
    shape = jax.ShapeDtypeStruct((blocks, depth, rows), F32)
    return pl.pallas_call(
        functools.partial(pack_kernel, chunks),
        out_shape=(shape, shape),
        in_specs=[ANY],
        out_specs=(VMEM, VMEM),
        scratch_shapes=[pltpu.VMEM(field.shape, F32), pltpu.SemaphoreType.DMA((chunks,))],
        name="pack_edges",
    )(field)


def forward_kernel(chunks, field, cross, coupling, following, left, right, g, h, f, ends, turned_left, sems):
    points, depth, rows = g.shape
    step = points // chunks
    group = min(rows, points)
    copies = []
    for n in range(chunks):
        span = pl.ds(n * step, step)
        for m, (source, target) in enumerate(((coupling, f), (field, g), (cross, h))):
            copy = pltpu.make_async_copy(source.at[span], target.at[span], sems.at[3 * n + m])
            copy.start()
            copies.append(copy)
    f[points] = following[...]
    for block in range(left.shape[0]):
        turned_left[block] = pltpu.roll(left[block], 2, 1)
    lanes = lane_index((depth, rows))
    planes = lax.broadcasted_iota(jnp.int32, (depth, rows), 0)

    def body(i, state):
        d, carried, unit, total, square = state
        x = g[i]
        block, k = i // group, lax.rem(i, group)
        later = jnp.where(k == rows - 1, 0, k + 1)
        edge = jnp.where(lanes == k, right[block], turned_left[block])
        edge = pltpu.roll(edge, rows - 1 - k, 1)
        beside = jnp.where(lanes == 0, edge, pltpu.roll(x, 1, 1))
        beside += jnp.where(lanes == rows - 1, edge, pltpu.roll(x, rows - 1, 1))
        beside += jnp.where(planes == 0, 0.0, pltpu.roll(x, 1, 0))
        beside += jnp.where(planes == depth - 1, 0.0, pltpu.roll(x, depth - 1, 0))
        y = (x + h[i] * (beside - 4.0 * x)) + carried
        above = f[i + 1]
        r = 1.0 / (d + above)
        factor = above * r
        part = y * r
        share = unit * r
        f[i] = factor
        g[i] = part
        h[i] = share
        return (
            1.0 + factor * d,
            factor * y,
            unit * factor,
            total + unit * part,
            square + unit * share,
        )

    zero = jnp.zeros((depth, rows), F32)
    state = None
    copies[0].wait()
    first = f[0]
    ends[0] = first
    state = (1.0 + first, zero, first, zero, zero)
    for n in range(chunks):
        if n > 0:
            copies[3 * n].wait()
        copies[3 * n + 1].wait()
        copies[3 * n + 2].wait()
        stop = (n + 1) * step if n + 1 == chunks else (n + 1) * step - 1
        start = max(n * step - 1, 0)
        state = lax.fori_loop(start, stop, body, state)
    d, carried, unit, total, square = state
    scale = 1.0 / ends[0]
    ends[0] = total * scale
    ends[1] = square * scale
    ends[2] = unit * scale
    ends[3] = g[points - 1]
    ends[4] = h[points - 1]
    ends[5] = f[points - 1]


def forward(field, cross, coupling, following, left, right):
    points, depth, rows = field.shape
    chunks = 16
    big = pltpu.VMEM((points, depth, rows), F32)
    return pl.pallas_call(
        functools.partial(forward_kernel, chunks),
        out_shape=(
            big,
            big,
            pltpu.VMEM((points + 1, depth, rows), F32),
            jax.ShapeDtypeStruct((6, depth, rows), F32),
        ),
        in_specs=[ANY, ANY, ANY, VMEM, VMEM, VMEM],
        out_specs=(VMEM, VMEM, VMEM, VMEM),
        scratch_shapes=[pltpu.VMEM(left.shape, F32), pltpu.SemaphoreType.DMA((3 * chunks,))],
        compiler_params=pltpu.CompilerParams(vmem_limit_bytes=8 << 20),
        name="forward",
    )(field, cross, coupling, following, left, right)


def backward_kernel(chunks, g, h, f, beside, out, held, sems):
    points = g.shape[0]
    step = points // chunks
    before = beside[0]

    def body(k, value, top):
        i = top - 1 - k
        value = f[i] * value + (g[i] + h[i] * before)
        held[i] = value
        return value

    value = beside[1]
    copies = []
    for n in reversed(range(chunks)):
        value = lax.fori_loop(0, step, functools.partial(body, top=(n + 1) * step), value, unroll=4)
        span = pl.ds(n * step, step)
        copy = pltpu.make_async_copy(held.at[span], out.at[span], sems.at[n])
        copy.start()
        copies.append(copy)
    for copy in copies:
        copy.wait()


def backward(g, h, f, beside):
    chunks = 16
    return pl.pallas_call(
        functools.partial(backward_kernel, chunks),
        out_shape=jax.ShapeDtypeStruct(g.shape, F32),
        in_specs=[VMEM, VMEM, VMEM, VMEM],
        out_specs=ANY,
        scratch_shapes=[pltpu.VMEM(g.shape, F32), pltpu.SemaphoreType.DMA((chunks,))],
        compiler_params=pltpu.CompilerParams(vmem_limit_bytes=12 << 20),
        name="backward",
    )(g, h, f, beside)


def join(a, b, e, q, p, t):
    count = a.shape[0]
    last, slope = q[0], t[0]
    heads, steep = [a[0]], [e[0]]
    lasts, slopes = [q[0]], [t[0]]
    for j in range(1, count):
        scale = 1.0 / (1.0 - b[j] * slope)
        head = (a[j] + b[j] * last) * scale
        climb = e[j] * scale
        reach = p[j] * slope
        last, slope = q[j] + p[j] * last + reach * head, t[j] + reach * climb
        heads.append(head)
        steep.append(climb)
        lasts.append(last)
        slopes.append(slope)
    following = jnp.zeros_like(a[0])
    before, after = [], []
    for j in reversed(range(count)):
        after.append(following)
        head = heads[j] + steep[j] * following
        before.append(lasts[j - 1] + slopes[j - 1] * head if j else jnp.zeros_like(head))
        following = head
    return jnp.stack([jnp.stack(before[::-1]), jnp.stack(after[::-1])])


def shards(field, cross, coupling):
    points, depth, rows = field.shape
    groups, sides = lax.axis_size("line"), lax.axis_size("row")
    low, high = pack_edges(field)
    left = lax.ppermute(high, "row", [(i, i + 1) for i in range(sides - 1)])
    right = lax.ppermute(low, "row", [(i + 1, i) for i in range(sides - 1)])
    following = lax.ppermute(coupling[0], "line", [((i + 1) % groups, i) for i in range(groups)])
    g, h, f, ends = forward(field, cross, coupling, following, left, right)
    packed = ends.reshape(6, groups, depth // groups, rows)
    gathered = lax.all_to_all(packed, "line", split_axis=1, concat_axis=1, tiled=True)
    pairs = join(*gathered)
    beside = lax.all_to_all(pairs, "line", split_axis=1, concat_axis=1, tiled=True)
    return backward(g, h, f, beside.reshape(2, depth, rows))


def solution(mesh):
    spec = P("line", None, "row")
    return jax.shard_map(
        shards, mesh=mesh, in_specs=(spec, spec, spec), out_specs=spec, check_vma=False
    )
```

```python
import functools

import jax
import jax.numpy as jnp
from jax import lax
from jax.experimental import pallas as pl
from jax.experimental.pallas import tpu as pltpu
from jax.sharding import PartitionSpec as P

F32 = jnp.float32
ANY = pl.BlockSpec(memory_space=pl.ANY)
VMEM = pl.BlockSpec(memory_space=pltpu.VMEM)


def lane_index(shape):
    return lax.broadcasted_iota(jnp.int32, shape, 1)


def join(a, b, e, q, p, t):
    count = len(a)
    last, slope = q[0], t[0]
    heads, steep = [a[0]], [e[0]]
    lasts, slopes = [q[0]], [t[0]]
    for j in range(1, count):
        scale = 1.0 / (1.0 - b[j] * slope)
        head = (a[j] + b[j] * last) * scale
        climb = e[j] * scale
        reach = p[j] * slope
        last, slope = q[j] + p[j] * last + reach * head, t[j] + reach * climb
        heads.append(head)
        steep.append(climb)
        lasts.append(last)
        slopes.append(slope)
    following = jnp.zeros_like(a[0])
    before, after = [], []
    for j in reversed(range(count)):
        after.append(following)
        head = heads[j] + steep[j] * following
        before.append(lasts[j - 1] + slopes[j - 1] * head if j else jnp.zeros_like(head))
        following = head
    return before[::-1], after[::-1]


def remote(source, target, send, recv, device):
    return pltpu.make_async_remote_copy(
        src_ref=source,
        dst_ref=target,
        send_sem=send,
        recv_sem=recv,
        device_id=device,
        device_id_type=pl.DeviceIdType.MESH,
    )


def fetch(source, target, sems, chunks):
    step = target.shape[0] // chunks
    copies = []
    for n in range(chunks):
        span = pl.ds(n * step, step)
        copies.append(pltpu.make_async_copy(source.at[span], target.at[span], sems.at[n]))
    return copies


def pack(held, low, high, copies):
    points, depth, rows = held.shape
    chunks = len(copies)
    step = points // chunks
    group = min(rows, points)
    lanes = lane_index((depth, rows))
    for n in range(chunks):
        copies[n].wait()
        base = n * step
        block, offset = base // group, base % group

        def body(k, state):
            first, last = state
            place = offset + k
            turned = pltpu.roll(held[base + k], place, 1)
            before = jnp.where(place == 0, rows - 1, place - 1)
            return jnp.where(lanes == place, turned, first), jnp.where(lanes == before, turned, last)

        if offset == 0:
            state = (jnp.zeros((depth, rows), F32), jnp.zeros((depth, rows), F32))
        state = lax.fori_loop(0, step, body, state, unroll=4)
        if offset + step == group:
            low[block], high[block] = state


def forward_kernel(
    chunks, groups, sides, field, cross, coupling, g, h, f, beside, held, inverse, low, high,
    left, right, following, ends, got, answer, land, field_sems, cross_sems, coupling_sems,
    edge_sems, out_send, out_recv, back_send, back_recv,
):
    points, depth, rows = g.shape
    step = points // chunks
    group = min(rows, points)
    part_depth = depth // groups
    me, side = lax.axis_index("line"), lax.axis_index("row")
    field_copies = fetch(field, g, field_sems, chunks)
    cross_copies = fetch(cross, held, cross_sems, chunks)
    coupling_copies = []
    for n in range(chunks):
        span = pl.ds(n * step, step)
        coupling_copies.append(
            pltpu.make_async_copy(coupling.at[span], f.at[span], coupling_sems.at[n])
        )
    for copy in field_copies + coupling_copies + cross_copies:
        copy.start()

    above_side = {"row": lax.rem(side + 1, sides)}
    below_side = {"row": lax.rem(side + sides - 1, sides)}
    peers = [lax.rem(me + o, groups) for o in range(1, groups)]
    barrier = pltpu.get_barrier_semaphore()
    for device in [{"line": peer} for peer in peers] + [above_side, below_side]:
        pl.semaphore_signal(barrier, inc=1, device_id=device, device_id_type=pl.DeviceIdType.MESH)
    pl.semaphore_wait(barrier, groups + 1)

    face = remote(coupling.at[0], following, edge_sems.at[0], edge_sems.at[1], {"line": peers[-1]})
    face.start()
    pack(g, low, high, field_copies)
    up = remote(high, left, edge_sems.at[2], edge_sems.at[3], above_side)
    down = remote(low, right, edge_sems.at[4], edge_sems.at[5], below_side)
    up.start()
    down.start()

    def factors(i, state):
        d, unit, square = state
        above = f[i + 1]
        r = 1.0 / (d + above)
        factor = above * r
        share = unit * r
        f[i] = factor
        inverse[i] = r
        h[i] = share
        return 1.0 + factor * d, unit * factor, square + unit * share

    zero = jnp.zeros((depth, rows), F32)
    coupling_copies[0].wait()
    first = f[0]
    beside[0] = first
    state = (1.0 + first, first, zero)
    for n in range(chunks):
        if n > 0:
            coupling_copies[n].wait()
        start = max(n * step - 1, 0)
        state = lax.fori_loop(start, (n + 1) * step - 1, factors, state)
    face.wait()
    f[points] = following[...]
    d, unit, square = factors(points - 1, state)
    scale = 1.0 / beside[0]

    def put(v, value):
        for j in range(groups):
            ends[j, v] = value[j * part_depth : (j + 1) * part_depth]

    put(1, square * scale)
    put(2, unit * scale)
    put(4, h[points - 1])
    put(5, f[points - 1])

    up.wait()
    down.wait()
    for block in range(left.shape[0]):
        left[block] = jnp.where(side == 0, 0.0, pltpu.roll(left[block], 2, 1))
        right[block] = jnp.where(side == sides - 1, 0.0, right[block])
    lanes = lane_index((depth, rows))
    planes = lax.broadcasted_iota(jnp.int32, (depth, rows), 0)

    def sources(i, state):
        carried, total = state
        x = g[i]
        block, k = i // group, lax.rem(i, group)
        edge = jnp.where(lanes == k, right[block], left[block])
        edge = pltpu.roll(edge, rows - 1 - k, 1)
        around = jnp.where(lanes == 0, edge, pltpu.roll(x, 1, 1))
        around += jnp.where(lanes == rows - 1, edge, pltpu.roll(x, rows - 1, 1))
        around += jnp.where(planes == 0, 0.0, pltpu.roll(x, 1, 0))
        around += jnp.where(planes == depth - 1, 0.0, pltpu.roll(x, depth - 1, 0))
        y = (x + held[i] * (around - 4.0 * x)) + carried
        g[i] = y * inverse[i]
        return f[i] * y, total + h[i] * y

    state = (zero, zero)
    for n in range(chunks):
        cross_copies[n].wait()
        state = lax.fori_loop(n * step, (n + 1) * step, sources, state)
    put(0, state[1] * (1.0 / beside[0]))
    put(3, g[points - 1])

    sent = []
    for o, peer in enumerate(peers):
        copy = remote(ends.at[peer], got.at[me], out_send.at[o], out_recv.at[o], {"line": peer})
        copy.start()
        sent.append(copy)
    got[me] = ends[me]
    for copy in sent:
        copy.wait()
    pairs = join(*[[got[j, v] for j in range(groups)] for v in range(6)])
    for j in range(groups):
        answer[j, 0] = pairs[0][j]
        answer[j, 1] = pairs[1][j]
    sent = []
    for o, peer in enumerate(peers):
        copy = remote(answer.at[peer], land.at[me], back_send.at[o], back_recv.at[o], {"line": peer})
        copy.start()
        sent.append(copy)
    land[me] = answer[me]
    for copy in sent:
        copy.wait()
    for j in range(groups):
        for v in range(2):
            beside[v, j * part_depth : (j + 1) * part_depth] = land[j, v]


def forward(field, cross, coupling):
    points, depth, rows = field.shape
    groups, sides = lax.axis_size("line"), lax.axis_size("row")
    chunks = 8
    big = pltpu.VMEM((points, depth, rows), F32)
    edge = pltpu.VMEM((max(1, points // rows), depth, rows), F32)
    part = depth // groups
    dma = pltpu.SemaphoreType.DMA
    return pl.pallas_call(
        functools.partial(forward_kernel, chunks, groups, sides),
        out_shape=(
            big,
            big,
            pltpu.VMEM((points + 1, depth, rows), F32),
            pltpu.VMEM((2, depth, rows), F32),
        ),
        in_specs=[ANY, ANY, ANY],
        out_specs=(VMEM, VMEM, VMEM, VMEM),
        scratch_shapes=[
            big,
            big,
            edge,
            edge,
            edge,
            edge,
            pltpu.VMEM((depth, rows), F32),
            pltpu.VMEM((groups, 6, part, rows), F32),
            pltpu.VMEM((groups, 6, part, rows), F32),
            pltpu.VMEM((groups, 2, part, rows), F32),
            pltpu.VMEM((groups, 2, part, rows), F32),
            dma((chunks,)),
            dma((chunks,)),
            dma((chunks,)),
            dma((6,)),
            dma((groups - 1,)),
            dma((groups - 1,)),
            dma((groups - 1,)),
            dma((groups - 1,)),
        ],
        compiler_params=pltpu.CompilerParams(
            vmem_limit_bytes=28 << 20, collective_id=0, has_side_effects=True
        ),
        name="forward",
    )(field, cross, coupling)


def backward_kernel(chunks, g, h, f, beside, out, held, sems):
    points = g.shape[0]
    step = points // chunks
    before = beside[0]

    def body(k, value, top):
        i = top - 1 - k
        value = f[i] * value + (g[i] + h[i] * before)
        held[i] = value
        return value

    value = beside[1]
    copies = []
    for n in reversed(range(chunks)):
        value = lax.fori_loop(0, step, functools.partial(body, top=(n + 1) * step), value, unroll=4)
        span = pl.ds(n * step, step)
        copy = pltpu.make_async_copy(held.at[span], out.at[span], sems.at[n])
        copy.start()
        copies.append(copy)
    for copy in copies:
        copy.wait()


def backward(g, h, f, beside):
    chunks = 16
    return pl.pallas_call(
        functools.partial(backward_kernel, chunks),
        out_shape=jax.ShapeDtypeStruct(g.shape, F32),
        in_specs=[VMEM, VMEM, VMEM, VMEM],
        out_specs=ANY,
        scratch_shapes=[pltpu.VMEM(g.shape, F32), pltpu.SemaphoreType.DMA((chunks,))],
        compiler_params=pltpu.CompilerParams(vmem_limit_bytes=12 << 20),
        name="backward",
    )(g, h, f, beside)


def shards(field, cross, coupling):
    return backward(*forward(field, cross, coupling))


def solution(mesh):
    spec = P("line", None, "row")
    return jax.shard_map(
        shards, mesh=mesh, in_specs=(spec, spec, spec), out_specs=spec, check_vma=False
    )
```
